128 devices in a mesh: row: 8 (over y, core), col: 16 (over z, x).
Axes of the slice: x: 4, y: 4, z: 4, core: 2. Of those that a mesh axis runs over, the one named last changes fastest.
Arguments:
- latents: bfloat16 [256, 16384], P('col', 'row'), may hold values from -30 to 30
- samples: bfloat16 [256, 65536], P('row', 'col'), may hold values from -30 to 30
- warm_dual: float32 [65536], P('col'), may hold values from -0.6 to 0.6
Outputs:
- targets: bfloat16 [256, 16384], P('col', 'row')
- pot_lat: float32 [16384], P('row')
- pot_tea: float32 [65536], P('col')
The draws below stay inside these ranges and needn't reach their ends.
All inputs are finite; a program needn't handle non-finite values.
Results may differ from the reference program's by a relative error of at most 0.012.
Values may be sent and summed in bfloat16 or wider, within the bound.
No kernel may reach another device: no remote copies, remote signals or barrier semaphores. Data moves between devices by JAX's collectives and lax.ppermute only.
A program may use at most 192 MiB of HBM per device.

```python
import math
import jax
import jax.numpy as jnp
from jax import lax

F = 256
CB = 4096
NLAT = 16384
NTEA = 65536
N_COL = 16


def feature_rows(key, count):
    values = jax.random.normal(jax.random.fold_in(key, 11), (F, count), jnp.float32)
    values = jnp.clip(values, -6.0, 6.0)
    return values.astype(jnp.bfloat16)


def draw_latents(key, part):
    return feature_rows(jax.random.fold_in(key, 1), NLAT)


def draw_samples(key, part):
    return feature_rows(jax.random.fold_in(key, 2), NTEA)


def steps_of(rng, shape, shards, low, high):
    factor_of = 1.0
    for position, shards_of in shards:
        steps = jax.random.uniform(jax.random.fold_in(jax.random.fold_in(rng, 6), position), (shards_of,), jnp.float32, low / len(shards), high / len(shards))
        factor_of = factor_of * jnp.repeat(jnp.exp(steps), shape[position] // shards_of).reshape((-1,) + (1,) * (len(shape) - 1 - position))
    return factor_of


def bell_draw(stream_key, dims, scale, reach, split=(), kind=jnp.bfloat16):
    gain = steps_of(stream_key, dims, split, -0.22, 0.18) if split else 1.0
    entries = jax.random.normal(stream_key, dims, jnp.float32) * scale * gain
    return jnp.minimum(jnp.maximum(entries, -reach), reach).astype(kind)


def setup_inputs(seed: int = 0) -> dict:
    arg_keys = jax.random.split(jax.random.key(seed), 4)
    latents = draw_latents(jax.random.fold_in(arg_keys[3], 71), 0)
    samples = draw_samples(jax.random.fold_in(arg_keys[3], 71), 0)
    warm_dual = bell_draw(arg_keys[2], (NTEA,), 0.1, 0.6, ((0, 16),), jnp.float32)
    return dict(latents=latents, samples=samples, warm_dual=warm_dual)


blur_scale = 0.04


def cost_rows(x_cols, y_all, y_norms):
    x_wide = x_cols.astype(jnp.float32)
    inner = lax.dot_general(x_wide, y_all, (((0,), (0,)), ((), ())), preferred_element_type=jnp.float32)
    x_norms = jnp.sum(x_wide * x_wide, axis=0)
    return (x_norms[:, None] + y_norms[None, :] - 2.0 * inner) / (2.0 * F)


def reference(latents, samples, warm_dual):
    latent_count = latents.shape[1]
    teacher_count = samples.shape[1]
    block_rows = min(512, latent_count)
    block_count = latent_count // block_rows
    y_all = samples.astype(jnp.float32)
    y_norms = jnp.sum(y_all * y_all, axis=0)
    stacked = jnp.transpose(latents.reshape(F, block_count, block_rows), (1, 0, 2))

    def dual_rows(x_cols):
        scores = (warm_dual[None, :] - cost_rows(x_cols, y_all, y_norms)) / blur_scale
        maximum = jnp.max(scores, axis=1)
        return maximum + jnp.log(jnp.sum(jnp.exp(scores - maximum[:, None]), axis=1))

    log_total = lax.map(dual_rows, stacked).reshape(latent_count)
    pot_lat = -blur_scale * (log_total - math.log(teacher_count))
    lat_blocks = pot_lat.reshape(block_count, block_rows)

    def dual_cols(packed):
        x_cols, f_rows = packed
        scores = (f_rows[:, None] - cost_rows(x_cols, y_all, y_norms)) / blur_scale
        maximum = jnp.max(scores, axis=0)
        return maximum, jnp.sum(jnp.exp(scores - maximum[None, :]), axis=0)

    maxima, totals = lax.map(dual_cols, (stacked, lat_blocks))
    highest = jnp.max(maxima, axis=0)
    summed = jnp.sum(totals * jnp.exp(maxima - highest[None, :]), axis=0)
    pot_tea = -blur_scale * (highest + jnp.log(summed) - math.log(latent_count))
    y_blocks = y_all.reshape(F, N_COL, CB)

    def barycenter(x_cols):
        scores = (pot_tea[None, :] - cost_rows(x_cols, y_all, y_norms)) / blur_scale
        scores = scores.reshape(block_rows, N_COL, CB)
        block_top = jnp.max(scores, axis=2)
        weights = jnp.exp(scores - block_top[:, :, None])
        den_parts = jnp.sum(weights, axis=2)
        low_weights = weights.astype(jnp.bfloat16).astype(jnp.float32)
        num_parts = jnp.einsum("bkc,fkc->bkf", low_weights, y_blocks)
        row_top = jnp.max(block_top, axis=1)
        factor = jnp.exp(block_top - row_top[:, None])
        denominator = jnp.sum(den_parts * factor, axis=1)
        numerator = jnp.sum(num_parts * factor[:, :, None], axis=1)
        return (numerator / denominator[:, None]).astype(jnp.bfloat16)

    targets = lax.map(barycenter, stacked).reshape(latent_count, F)
    return jnp.transpose(targets), pot_lat, pot_tea
```

```python
import functools
import math

import jax
import jax.numpy as jnp
from jax import lax
from jax.experimental import pallas as pl
from jax.experimental.pallas import tpu as pltpu
from jax.sharding import PartitionSpec as P

BLUR = 0.04
LOG2E = 1.0 / math.log(2.0)
LN2 = math.log(2.0)
LOW, HIGH = 2.0**-90, 2.0**120
CHUNK = 256
TILE = 512
LANES = 128

VMEM = pl.BlockSpec(memory_space=pltpu.VMEM)
SMEM = pl.BlockSpec(memory_space=pltpu.SMEM)
PARAMS = pltpu.CompilerParams(vmem_limit_bytes=48 * 1024 * 1024)


def dot(a, b, ca, cb):
    return lax.dot_general(
        a, b, (((ca,), (cb,)), ((), ())), preferred_element_type=jnp.float32
    )


def place(core_ref, own_ref, sib_ref, y_all):
    core = core_ref[0]
    piece = 32
    for k in range(own_ref.shape[0] // piece):
        rows = slice(k * piece, (k + 1) * piece)
        mine = pl.multiple_of((2 * k + core) * piece, piece)
        other = pl.multiple_of((2 * k + 1 - core) * piece, piece)
        y_all[pl.ds(mine, piece), :] = own_ref[rows, :]
        y_all[pl.ds(other, piece), :] = sib_ref[rows, :]


def square_sums(ref, width):
    parts = []
    for j in range(0, ref.shape[1], width):
        v = ref[:256, j : j + width].astype(jnp.float32)
        parts.append(jnp.sum(v * v, axis=0, keepdims=True))
    return parts


def lse2(stacked):
    top = jnp.max(stacked, axis=0, keepdims=True)
    return top + jnp.log2(jnp.sum(jnp.exp2(stacked - top), axis=0, keepdims=True))


def columns_of(row_ref, col_ref):
    for i in range(0, row_ref.shape[1], LANES):
        block = jnp.broadcast_to(row_ref[0:1, i : i + LANES], (LANES, LANES))
        col_ref[i : i + LANES, :] = block.T


def row_pass(scale, core_ref, x_ref, own_ref, sib_ref, warm_ref, out_ref, yn_ref, y_all, beta, sums, tops):
    rows, cols = x_ref.shape[1], own_ref.shape[1]
    place(core_ref, own_ref, sib_ref, y_all)
    for j, part in enumerate(square_sums(y_all, TILE)):
        sl = slice(j * TILE, (j + 1) * TILE)
        yn_ref[0:1, sl] = part
        beta[0:1, sl] = warm_ref[0:1, sl] * (LOG2E / BLUR) - part * (0.5 * scale)
    sample = dot(x_ref[:, :LANES].T, y_all[:, :TILE], 1, 0) * scale + beta[0:1, :TILE]
    shift = jnp.max(sample)

    def chunk(c, _):
        base = pl.multiple_of(c * CHUNK, CHUNK)
        xt = x_ref[:, pl.ds(base, CHUNK)].T
        acc = None
        for j in range(0, cols, TILE):
            b = beta[0:1, j : j + TILE] - shift
            e = jnp.exp2(dot(xt, y_all[:, j : j + TILE], 1, 0) * scale + b)
            part = e[:, :LANES]
            for k in range(LANES, TILE, LANES):
                part = part + e[:, k : k + LANES]
            acc = part if acc is None else acc + part
        sums[pl.ds(base, CHUNK), :] = acc
        return 0

    lax.fori_loop(0, rows // CHUNK, chunk, 0)
    good = []
    for i in range(0, rows, LANES):
        s = jnp.sum(sums[i : i + LANES, :].T, axis=0, keepdims=True)
        good.append(jnp.where((s > LOW) & (s < HIGH), 1.0, 0.0))
        out_ref[:, i : i + LANES] = jnp.broadcast_to(shift + jnp.log2(s), (out_ref.shape[0], LANES))
    ok = functools.reduce(jnp.minimum, good)

    @pl.when(jnp.min(ok) < 0.5)
    def _():
        def slow(c, _):
            base = pl.multiple_of(c * LANES, LANES)
            xt = x_ref[:, pl.ds(base, LANES)].T

            def tile(j, state):
                top, total = state
                lane = pl.multiple_of(j * LANES, LANES)
                t = dot(xt, y_all[:, pl.ds(lane, LANES)], 1, 0) * scale + beta[0:1, pl.ds(lane, LANES)]
                new = jnp.maximum(top, t)
                return new, total * jnp.exp2(top - new) + jnp.exp2(t - new)

            first = jnp.full((LANES, LANES), -1e30, jnp.float32)
            top, total = lax.fori_loop(0, cols // LANES, tile, (first, jnp.zeros_like(first)))
            top, total = top.T, total.T
            high = jnp.max(top, axis=0, keepdims=True)
            s = jnp.sum(total * jnp.exp2(top - high), axis=0, keepdims=True)
            out_ref[:, pl.ds(base, LANES)] = jnp.broadcast_to(high + jnp.log2(s), (out_ref.shape[0], LANES))
            return 0

        lax.fori_loop(0, rows // LANES, slow, 0)


def col_pass(scale, count, core_ref, x_ref, own_ref, sib_ref, lg_ref, out_ref, l_ref, pot_ref, y_all, x_t, l_col):
    rows, cols = x_ref.shape[1], own_ref.shape[1]
    place(core_ref, own_ref, sib_ref, y_all)
    l_ref[...] = lse2(lg_ref[...])
    columns_of(l_ref, l_col)
    for j, part in enumerate(square_sums(x_ref, TILE)):
        sl = slice(j * TILE, (j + 1) * TILE)
        pot_ref[0:1, sl] = part / 512.0 - (BLUR * LN2) * l_ref[0:1, sl] + BLUR * math.log(count)
    for i in range(0, rows, CHUNK):
        x_t[i : i + CHUNK, :] = x_ref[:, i : i + CHUNK].T
    sample = dot(x_t[:CHUNK, :], y_all[:, :LANES], 1, 0) * scale - l_col[:CHUNK, :]
    shift = jnp.max(sample)

    def tile(j, ok):
        lane = pl.multiple_of(j * TILE, TILE)
        y_tile = y_all[:, pl.ds(lane, TILE)]
        accs = [None] * (TILE // LANES)
        for i in range(0, rows, CHUNK):
            g = dot(x_t[i : i + CHUNK, :], y_tile, 1, 0)
            b = l_col[i : i + CHUNK, :] + shift
            for k in range(TILE // LANES):
                e = jnp.exp2(g[:, k * LANES : (k + 1) * LANES] * scale - b)
                part = jnp.sum(e.reshape(CHUNK // 8, 8, LANES), axis=0)
                accs[k] = part if accs[k] is None else accs[k] + part
        for k in range(TILE // LANES):
            s = jnp.sum(accs[k], axis=0, keepdims=True)
            ok = jnp.minimum(ok, jnp.where((s > LOW) & (s < HIGH), 1.0, 0.0))
            out_ref[:, pl.ds(lane + k * LANES, LANES)] = jnp.broadcast_to(shift + jnp.log2(s), (out_ref.shape[0], LANES))
        return ok

    ok = lax.fori_loop(0, cols // TILE, tile, jnp.ones((1, LANES), jnp.float32))

    @pl.when(jnp.min(ok) < 0.5)
    def _():
        def slow(j, _):
            lane = pl.multiple_of(j * LANES, LANES)
            y_tile = y_all[:, pl.ds(lane, LANES)]

            def rows_of(c, state):
                top, total = state
                base = pl.multiple_of(c * LANES, LANES)
                t = dot(x_t[pl.ds(base, LANES), :], y_tile, 1, 0) * scale - l_col[pl.ds(base, LANES), :]
                new = jnp.maximum(top, t)
                return new, total * jnp.exp2(top - new) + jnp.exp2(t - new)

            first = jnp.full((LANES, LANES), -1e30, jnp.float32)
            top, total = lax.fori_loop(0, rows // LANES, rows_of, (first, jnp.zeros_like(first)))
            high = jnp.max(top, axis=0, keepdims=True)
            s = jnp.sum(total * jnp.exp2(top - high), axis=0, keepdims=True)
            out_ref[:, pl.ds(lane, LANES)] = jnp.broadcast_to(high + jnp.log2(s), (out_ref.shape[0], LANES))
            return 0

        lax.fori_loop(0, cols // LANES, slow, 0)


def mean_pass(scale, ratio, count, core_ref, x_ref, own_ref, sib_ref, mg_ref, l_ref, yn_ref, out_ref, pot_ref, y_all, l_col, bias, w_even, w_odd, den):
    rows, cols = x_ref.shape[1], own_ref.shape[1]
    features = x_ref.shape[0]
    place(core_ref, own_ref, sib_ref, y_all)
    y_all[features:, :] = jnp.ones((y_all.shape[0] - features, cols), y_all.dtype)
    m = lse2(mg_ref[...])
    pot_ref[...] = yn_ref[...] / 512.0 - (BLUR * LN2) * (m + ratio)
    bias[...] = math.log2(count) - m
    columns_of(l_ref, l_col)

    def weigh(c, w):
        base = pl.multiple_of(c * CHUNK, CHUNK)
        xt = x_ref[:, pl.ds(base, CHUNK)].T
        lc = l_col[pl.ds(base, CHUNK), :]
        for j in range(0, cols, TILE):
            g = dot(xt, y_all[:features, j : j + TILE], 1, 0)
            for k in range(0, TILE, LANES):
                t = g[:, k : k + LANES] * scale + (bias[0:1, j + k : j + k + LANES] - lc)
                w[:, j + k : j + k + LANES] = jnp.exp2(t).astype(jnp.bfloat16)

    def gather(c, w):
        base = pl.multiple_of(c * CHUNK, CHUNK)
        num = dot(y_all[...], w[...], 1, 1)
        out_ref[:, pl.ds(base, CHUNK)] = num[:features].astype(jnp.bfloat16)
        den[0:1, pl.ds(base, CHUNK)] = num[features : features + 1]

    last = rows // CHUNK - 1
    weigh(0, w_even)

    def pair(h, _):
        c = 2 * h
        weigh(c + 1, w_odd)
        gather(c, w_even)
        weigh(jnp.minimum(c + 2, last), w_even)
        gather(c + 1, w_odd)
        return 0

    lax.fori_loop(0, rows // CHUNK // 2, pair, 0)
    share = out_ref.shape[0] // 16
    width = rows // 8
    high = den[...].astype(jnp.bfloat16).astype(jnp.float32)
    low = den[...] - high
    grid = jnp.concatenate(
        [v[0:1, k * width : (k + 1) * width] for v in (high, low) for k in range(8)], axis=0
    ).astype(jnp.bfloat16)
    for k in range(out_ref.shape[0] // share):
        out_ref[k * share : (k + 1) * share, rows : rows + width] = grid


def finish(rows, in_ref, out_ref):
    share = out_ref.shape[0]
    width = rows // 8
    total = None
    for k in range(in_ref.shape[0] // share):
        part = in_ref[k * share : (k + 1) * share, :].astype(jnp.float32)
        total = part if total is None else total + part
    den = total[:8, rows:] + total[8:16, rows:]
    for k in range(8):
        sl = slice(k * width, (k + 1) * width)
        out_ref[:, sl] = (total[:, sl] / den[k : k + 1, :]).astype(jnp.bfloat16)


def per_device(latents, samples, warm_dual):
    n_row, n_col = lax.axis_size("row"), lax.axis_size("col")
    rows, cols = latents.shape[1], samples.shape[1]
    features = latents.shape[0] * n_col
    all_rows, all_cols = rows * n_row, cols * n_col
    scale = 2.0 * LOG2E / (2.0 * features * BLUR)
    f32, b16 = jnp.float32, jnp.bfloat16
    core = (lax.axis_index("row") % 2).astype(jnp.int32).reshape(1)

    def spread(v, axis, n, **kw):
        return lax.all_to_all(jnp.tile(v, (n, 1)), axis, 0, 0, tiled=True, **kw)

    groups = [[2 * k + c for k in range(n_row // 2)] for c in range(2)]
    own = spread(samples, "row", n_row // 2, axis_index_groups=groups)
    x = spread(latents, "col", n_col)
    sib = lax.ppermute(own, "row", [(s, s ^ 1) for s in range(n_row)])

    y_scratch = pltpu.VMEM((features, cols), b16)
    l_part, yn = pl.pallas_call(
        functools.partial(row_pass, scale),
        out_shape=[jax.ShapeDtypeStruct((n_col, rows), f32), jax.ShapeDtypeStruct((1, cols), f32)],
        in_specs=[SMEM, VMEM, VMEM, VMEM, VMEM],
        out_specs=[VMEM, VMEM],
        scratch_shapes=[y_scratch, pltpu.VMEM((1, cols), f32), pltpu.VMEM((rows, LANES), f32), pltpu.VMEM((rows, LANES), f32)],
        compiler_params=PARAMS,
        name="row_pass",
    )(core, x, own, sib, warm_dual.reshape(1, cols))
    l_all = lax.all_to_all(l_part, "col", 0, 0, tiled=True)
    m_part, l_sum, pot_lat = pl.pallas_call(
        functools.partial(col_pass, scale, all_cols),
        out_shape=[jax.ShapeDtypeStruct((n_row, cols), f32), jax.ShapeDtypeStruct((1, rows), f32), jax.ShapeDtypeStruct((1, rows), f32)],
        in_specs=[SMEM, VMEM, VMEM, VMEM, VMEM],
        out_specs=[VMEM, VMEM, VMEM],
        scratch_shapes=[y_scratch, pltpu.VMEM((rows, features), b16), pltpu.VMEM((rows, LANES), f32)],
        compiler_params=PARAMS,
        name="col_pass",
    )(core, x, own, sib, l_all)
    m_all = lax.all_to_all(m_part, "row", 0, 0, tiled=True)
    num, pot_tea = pl.pallas_call(
        functools.partial(mean_pass, scale, math.log2(all_cols / all_rows), all_rows),
        out_shape=[jax.ShapeDtypeStruct((features, rows + rows // 8), b16), jax.ShapeDtypeStruct((1, cols), f32)],
        in_specs=[SMEM, VMEM, VMEM, VMEM, VMEM, VMEM, VMEM],
        out_specs=[VMEM, VMEM],
        scratch_shapes=[
            pltpu.VMEM((features + 16, cols), b16),
            pltpu.VMEM((rows, LANES), f32),
            pltpu.VMEM((1, cols), f32),
            pltpu.VMEM((CHUNK, cols), b16),
            pltpu.VMEM((CHUNK, cols), b16),
            pltpu.VMEM((1, rows), f32),
        ],
        compiler_params=PARAMS,
        name="mean_pass",
    )(core, x, own, sib, m_all, l_sum, yn)
    got = lax.all_to_all(num, "col", 0, 0, tiled=True)
    targets = pl.pallas_call(
        functools.partial(finish, rows),
        out_shape=jax.ShapeDtypeStruct((features // n_col, rows), b16),
        in_specs=[VMEM],
        out_specs=VMEM,
        name="finish",
    )(got)
    return targets, pot_lat.reshape(rows), pot_tea.reshape(cols)


def solution(mesh):
    return jax.shard_map(
        per_device,
        mesh=mesh,
        in_specs=(P("col", "row"), P("row", "col"), P("col")),
        out_specs=(P("col", "row"), P("row"), P("col")),
        check_vma=False,
    )
```

```python
import functools
import math

import jax
import jax.numpy as jnp
import numpy as np
from jax import lax
from jax.experimental import pallas as pl
from jax.experimental.pallas import tpu as pltpu
from jax.sharding import PartitionSpec as P

BLUR = 0.04
LOG2E = 1.0 / math.log(2.0)
LN2 = math.log(2.0)
LOW, HIGH = 2.0**-40, 2.0**40
CHUNK = 256
BIG = 512
TILE = 512
LANES = 128

VMEM = pl.BlockSpec(memory_space=pltpu.VMEM)
SMEM = pl.BlockSpec(memory_space=pltpu.SMEM)


def params(mib):
    return pltpu.CompilerParams(vmem_limit_bytes=mib * 1024 * 1024)


def dot(a, b, ca, cb):
    return lax.dot_general(
        a, b, (((ca,), (cb,)), ((), ())), preferred_element_type=jnp.float32
    )


def assemble(place_ref, pieces, y_all):
    for k, piece in enumerate(pieces):
        height = piece.shape[0]
        row = pl.multiple_of(place_ref[k], 16)
        y_all[pl.ds(row, height), :] = piece[...]


def load(y_ref, y_all):
    y_all[: y_ref.shape[0], :] = y_ref[...]


def square_sums(ref, width):
    parts = []
    for j in range(0, ref.shape[1], width):
        v = ref[:256, j : j + width].astype(jnp.float32)
        parts.append(jnp.sum(v * v, axis=0, keepdims=True))
    return parts


def lse2(stacked):
    top = jnp.max(stacked, axis=0, keepdims=True)
    return top + jnp.log2(jnp.sum(jnp.exp2(stacked - top), axis=0, keepdims=True))


def columns_of(row_ref, col_ref):
    for i in range(0, row_ref.shape[1], LANES):
        block = jnp.broadcast_to(row_ref[0:1, i : i + LANES], (LANES, LANES))
        col_ref[i : i + LANES, :] = block.T.astype(col_ref.dtype)


def in_range(s):
    return jnp.where((s > LOW) & (s < HIGH), 1.0, 0.0)


def row_pass(scale, place_ref, x_ref, warm_ref, *refs):
    *pieces, out_ref, yn_ref, beta, y_ref, e_ref, aux_ref, y_all, sums = refs
    rows, cols = x_ref.shape[1], y_ref.shape[1]
    assemble(place_ref, pieces, y_all)
    y_ref[...] = y_all[...]
    for j, part in enumerate(square_sums(y_all, TILE)):
        sl = slice(j * TILE, (j + 1) * TILE)
        yn_ref[0:1, sl] = part
        beta[0:1, sl] = warm_ref[0:1, sl] * (LOG2E / BLUR) - part * (0.5 * scale)
    sample = dot(x_ref[:, :LANES].T, y_all[:, :TILE], 1, 0) * scale + beta[0:1, :TILE]
    shift = jnp.max(sample)

    def chunk(c, _):
        base = pl.multiple_of(c * BIG, BIG)
        xt = x_ref[:, pl.ds(base, BIG)].T
        acc = None
        for j in range(0, cols, TILE):
            b = beta[0:1, j : j + TILE] - shift
            e = jnp.exp2(dot(xt, y_all[:, j : j + TILE], 1, 0) * scale + b)
            e_ref[pl.ds(base, BIG), j : j + TILE] = e.astype(jnp.bfloat16)
            part = e[:, :LANES]
            for k in range(LANES, TILE, LANES):
                part = part + e[:, k : k + LANES]
            acc = part if acc is None else acc + part
        sums[pl.ds(base, BIG), :] = acc
        return 0

    lax.fori_loop(0, rows // BIG, chunk, 0)
    good = []
    for i in range(0, rows, LANES):
        s = jnp.sum(sums[i : i + LANES, :].T, axis=0, keepdims=True)
        good.append(in_range(s))
        out_ref[:, i : i + LANES] = jnp.broadcast_to(shift + jnp.log2(s), (out_ref.shape[0], LANES))
    ok = jnp.min(functools.reduce(jnp.minimum, good))
    aux_ref[0:1, :] = jnp.full((1, LANES), shift, jnp.float32)
    aux_ref[1:2, :] = jnp.full((1, LANES), ok, jnp.float32)

    @pl.when(ok < 0.5)
    def _():
        def slow(c, _):
            base = pl.multiple_of(c * LANES, LANES)
            xt = x_ref[:, pl.ds(base, LANES)].T

            def tile(j, state):
                top, total = state
                lane = pl.multiple_of(j * LANES, LANES)
                t = dot(xt, y_all[:, pl.ds(lane, LANES)], 1, 0) * scale + beta[0:1, pl.ds(lane, LANES)]
                new = jnp.maximum(top, t)
                return new, total * jnp.exp2(top - new) + jnp.exp2(t - new)

            first = jnp.full((LANES, LANES), -1e30, jnp.float32)
            top, total = lax.fori_loop(0, cols // LANES, tile, (first, jnp.zeros_like(first)))
            top, total = top.T, total.T
            high = jnp.max(top, axis=0, keepdims=True)
            s = jnp.sum(total * jnp.exp2(top - high), axis=0, keepdims=True)
            out_ref[:, pl.ds(base, LANES)] = jnp.broadcast_to(high + jnp.log2(s), (out_ref.shape[0], LANES))
            return 0

        lax.fori_loop(0, rows // LANES, slow, 0)


def col_pass(scale, count, x_ref, y_ref, e_ref, lg_ref, beta_ref, aux_ref, out_ref, l_ref, u_ref, pot_ref, flag_ref, u_col, l_col, total):
    rows, cols = x_ref.shape[1], y_ref.shape[1]
    l_ref[...] = lse2(lg_ref[...])
    u_ref[...] = jnp.exp2(aux_ref[0:1, 0:1] - l_ref[...])
    columns_of(u_ref, u_col)
    for j, part in enumerate(square_sums(x_ref, TILE)):
        sl = slice(j * TILE, (j + 1) * TILE)
        pot_ref[0:1, sl] = part / 512.0 - (BLUR * LN2) * l_ref[0:1, sl] + BLUR * math.log(count)

    total[...] = jnp.zeros_like(total)

    def block(i, _):
        base = pl.multiple_of(i * LANES, LANES)
        u = u_col[pl.ds(base, LANES), :]
        u = jnp.concatenate([u, u], axis=1)
        for j in range(0, cols, 2 * LANES):
            p = e_ref[pl.ds(base, LANES), j : j + 2 * LANES] * u
            while p.shape[0] > 8:
                p = p[: p.shape[0] // 2] + p[p.shape[0] // 2 :]
            total[:, j : j + 2 * LANES] += p.astype(jnp.float32)
        return 0

    lax.fori_loop(0, rows // LANES, block, 0)
    s = jnp.sum(total[...], axis=0, keepdims=True)
    ok = jnp.minimum(jnp.min(in_range(s)), jnp.min(aux_ref[1:2, :]))
    out_ref[...] = jnp.broadcast_to(jnp.log2(s) - beta_ref[...], out_ref.shape)
    flag_ref[...] = jnp.full((1, LANES), ok, jnp.float32)

    @pl.when(ok < 0.5)
    def _():
        columns_of(l_ref, l_col)

        def slow(j, _):
            lane = pl.multiple_of(j * LANES, LANES)
            y_tile = y_ref[:, pl.ds(lane, LANES)]

            def rows_of(c, state):
                top, total = state
                base = pl.multiple_of(c * LANES, LANES)
                t = dot(x_ref[:, pl.ds(base, LANES)].T, y_tile, 1, 0) * scale - l_col[pl.ds(base, LANES), :]
                new = jnp.maximum(top, t)
                return new, total * jnp.exp2(top - new) + jnp.exp2(t - new)

            first = jnp.full((LANES, LANES), -1e30, jnp.float32)
            top, total = lax.fori_loop(0, rows // LANES, rows_of, (first, jnp.zeros_like(first)))
            high = jnp.max(top, axis=0, keepdims=True)
            s = jnp.sum(total * jnp.exp2(top - high), axis=0, keepdims=True)
            out_ref[:, pl.ds(lane, LANES)] = jnp.broadcast_to(high + jnp.log2(s), (out_ref.shape[0], LANES))
            return 0

        lax.fori_loop(0, cols // LANES, slow, 0)


def mean_pass(scale, ratio, count, x_ref, y_ref, e_ref, mg_ref, l_ref, u_ref, beta_ref, yn_ref, flag_ref, out_ref, pot_ref, y_all, l_col, bias, w, den):
    rows, cols = x_ref.shape[1], y_ref.shape[1]
    features = x_ref.shape[0]
    m = lse2(mg_ref[...])
    pot_ref[...] = yn_ref[...] / 512.0 - (BLUR * LN2) * (m + ratio)
    bias[...] = math.log2(count) - m
    which = lax.broadcasted_iota(jnp.int32, (16, TILE), 0)
    for j in range(0, cols, TILE):
        sl = slice(j, j + TILE)
        v = jnp.exp2(bias[0:1, sl] - beta_ref[0:1, sl])
        y_all[:features, sl] = (y_ref[:, sl].astype(jnp.float32) * v).astype(jnp.bfloat16)
        high = v.astype(jnp.bfloat16).astype(jnp.float32)
        y_all[features:, sl] = jnp.where(which == 0, high, jnp.where(which == 1, v - high, 0.0)).astype(jnp.bfloat16)

    def chunk(c, _):
        sl = pl.ds(pl.multiple_of(c * CHUNK, CHUNK), CHUNK)
        u = u_ref[0:1, sl]
        num = dot(y_all[...], e_ref[sl, :], 1, 1)
        out_ref[:, sl] = (num[:features] * u).astype(jnp.bfloat16)
        den[0:1, sl] = (num[features : features + 1] + num[features + 1 : features + 2]) * u
        return 0

    lax.fori_loop(0, rows // CHUNK, chunk, 0)

    @pl.when(jnp.min(flag_ref[...]) < 0.5)
    def _():
        columns_of(l_ref, l_col)
        y_all[:features, :] = y_ref[...]
        y_all[features:, :] = jnp.ones((y_all.shape[0] - features, cols), y_all.dtype)

        def slow(c, _):
            sl = pl.ds(pl.multiple_of(c * CHUNK, CHUNK), CHUNK)
            xt = x_ref[:, sl].T

            def tile(j, _):
                lane = pl.ds(pl.multiple_of(j * LANES, LANES), LANES)
                g = dot(xt, y_all[:features, lane], 1, 0)
                w[:, lane] = jnp.exp2(g * scale + (bias[0:1, lane] - l_col[sl, :])).astype(jnp.bfloat16)
                return 0

            lax.fori_loop(0, cols // LANES, tile, 0)
            num = dot(y_all[...], w[...], 1, 1)
            out_ref[:, sl] = num[:features].astype(jnp.bfloat16)
            den[0:1, sl] = num[features : features + 1]
            return 0

        lax.fori_loop(0, rows // CHUNK, slow, 0)

    share = out_ref.shape[0] // 16
    width = rows // 8
    high = den[...].astype(jnp.bfloat16).astype(jnp.float32)
    low = den[...] - high
    grid = jnp.concatenate(
        [v[0:1, k * width : (k + 1) * width] for v in (high, low) for k in range(8)], axis=0
    ).astype(jnp.bfloat16)
    for k in range(out_ref.shape[0] // share):
        out_ref[k * share : (k + 1) * share, rows : rows + width] = grid


def finish(rows, in_ref, out_ref):
    share = out_ref.shape[0]
    width = rows // 8
    total = None
    for k in range(in_ref.shape[0] // share):
        part = in_ref[k * share : (k + 1) * share, :].astype(jnp.float32)
        total = part if total is None else total + part
    den = total[:8, rows:] + total[8:16, rows:]
    for k in range(8):
        sl = slice(k * width, (k + 1) * width)
        out_ref[:, sl] = (total[:, sl] / den[k : k + 1, :]).astype(jnp.bfloat16)


def per_device(latents, samples, warm_dual):
    n_row, n_col = lax.axis_size("row"), lax.axis_size("col")
    rows, cols = latents.shape[1], samples.shape[1]
    features = latents.shape[0] * n_col
    all_rows, all_cols = rows * n_row, cols * n_col
    scale = 2.0 * LOG2E / (2.0 * features * BLUR)
    f32, b16 = jnp.float32, jnp.bfloat16
    ring = n_row // 2
    share = samples.shape[0]
    half = share // 2

    def along(v, step):
        return lax.ppermute(v, "row", [(s, (s + 2 * step) % n_row) for s in range(n_row)])

    def swap(v):
        return lax.ppermute(v, "row", [(s, s ^ 1) for s in range(n_row)])

    low, high = samples[:half], samples[half:]
    left, left_high = along(low, 1), along(high, 1)
    right_low, right = along(low, -1), along(high, -1)
    far_low, far_high = along(left, 1), along(right, -1)
    pieces = [low, high, left, left_high, right_low, right, far_low, far_high]
    steps = [0, 0, -1, -1, 1, 1, 2, 2]
    table = np.zeros((n_row, 2 * len(steps)), np.int32)
    for r in range(n_row):
        for k, step in enumerate(steps):
            slot = ((r // 2 + step) % ring) * 2
            table[r, k] = (slot + r % 2) * share + (k % 2) * half
            table[r, k + len(steps)] = (slot + 1 - r % 2) * share + (k % 2) * half
    at = lax.dynamic_index_in_dim(jnp.asarray(table), lax.axis_index("row"), 0, keepdims=False)
    pieces = pieces + [swap(p) for p in pieces]
    x = lax.all_to_all(jnp.tile(latents, (n_col, 1)), "col", 0, 0, tiled=True)

    def like(*shape, dtype=f32):
        return jax.ShapeDtypeStruct(shape, dtype)

    l_part, yn, beta, y, e, aux = pl.pallas_call(
        functools.partial(row_pass, scale),
        out_shape=[
            like(n_col, rows),
            like(1, cols),
            like(1, cols),
            like(features, cols, dtype=b16),
            like(rows, cols, dtype=b16),
            like(2, LANES),
        ],
        in_specs=[SMEM] + [VMEM] * (2 + len(pieces)),
        out_specs=[VMEM] * 6,
        scratch_shapes=[pltpu.VMEM((features, cols), b16), pltpu.VMEM((rows, LANES), f32)],
        compiler_params=params(12),
        name="row_pass",
    )(at, x, warm_dual.reshape(1, cols), *pieces)
    l_all = lax.all_to_all(l_part, "col", 0, 0, tiled=True)
    m_part, l_sum, u, pot_lat, flag = pl.pallas_call(
        functools.partial(col_pass, scale, all_cols),
        out_shape=[like(n_row, cols), like(1, rows), like(1, rows), like(1, rows), like(1, LANES)],
        in_specs=[VMEM] * 6,
        out_specs=[VMEM] * 5,
        scratch_shapes=[pltpu.VMEM((rows, LANES), b16), pltpu.VMEM((rows, LANES), f32), pltpu.VMEM((8, cols), f32)],
        compiler_params=params(8),
        name="col_pass",
    )(x, y, e, l_all, beta, aux)
    m_all = lax.all_to_all(m_part, "row", 0, 0, tiled=True)
    num, pot_tea = pl.pallas_call(
        functools.partial(mean_pass, scale, math.log2(all_cols / all_rows), all_rows),
        out_shape=[like(features, rows + rows // 8, dtype=b16), like(1, cols)],
        in_specs=[VMEM] * 9,
        out_specs=[VMEM] * 2,
        scratch_shapes=[
            pltpu.VMEM((features + 16, cols), b16),
            pltpu.VMEM((rows, LANES), f32),
            pltpu.VMEM((1, cols), f32),
            pltpu.VMEM((CHUNK, cols), b16),
            pltpu.VMEM((1, rows), f32),
        ],
        compiler_params=params(12),
        name="mean_pass",
    )(x, y, e, m_all, l_sum, u, beta, yn, flag)
    got = lax.all_to_all(num, "col", 0, 0, tiled=True)
    targets = pl.pallas_call(
        functools.partial(finish, rows),
        out_shape=jax.ShapeDtypeStruct((features // n_col, rows), b16),
        in_specs=[VMEM],
        out_specs=VMEM,
        name="finish",
    )(got)
    return targets, pot_lat.reshape(rows), pot_tea.reshape(cols)


def solution(mesh):
    return jax.shard_map(
        per_device,
        mesh=mesh,
        in_specs=(P("col", "row"), P("row", "col"), P("col")),
        out_specs=(P("col", "row"), P("row"), P("col")),
        check_vma=False,
    )
```

```python
import functools
import math

import jax
import jax.numpy as jnp
import numpy as np
from jax import lax
from jax.experimental import pallas as pl
from jax.experimental.pallas import tpu as pltpu
from jax.sharding import PartitionSpec as P

BLUR = 0.04
LOG2E = 1.0 / math.log(2.0)
LN2 = math.log(2.0)
LOW, HIGH = 2.0**-40, 2.0**40
CHUNK = 256
BIG = 512
TILE = 512
LANES = 128

VMEM = pl.BlockSpec(memory_space=pltpu.VMEM)
SMEM = pl.BlockSpec(memory_space=pltpu.SMEM)


def params(mib):
    return pltpu.CompilerParams(vmem_limit_bytes=mib * 1024 * 1024)


def dot(a, b, ca, cb):
    return lax.dot_general(
        a, b, (((ca,), (cb,)), ((), ())), preferred_element_type=jnp.float32
    )


def assemble(place_ref, pieces, y_all):
    for k, piece in enumerate(pieces):
        height = piece.shape[0]
        row = pl.multiple_of(place_ref[k], 16)
        y_all[pl.ds(row, height), :] = piece[...]


def load(y_ref, y_all):
    y_all[: y_ref.shape[0], :] = y_ref[...]


def square_sums(ref, width):
    parts = []
    for j in range(0, ref.shape[1], width):
        v = ref[:256, j : j + width].astype(jnp.float32)
        parts.append(jnp.sum(v * v, axis=0, keepdims=True))
    return parts


def lse2(stacked):
    top = jnp.max(stacked, axis=0, keepdims=True)
    return top + jnp.log2(jnp.sum(jnp.exp2(stacked - top), axis=0, keepdims=True))


def columns_of(row_ref, col_ref):
    for i in range(0, row_ref.shape[1], LANES):
        block = jnp.broadcast_to(row_ref[0:1, i : i + LANES], (LANES, LANES))
        col_ref[i : i + LANES, :] = block.T.astype(col_ref.dtype)


def in_range(s):
    return jnp.where((s > LOW) & (s < HIGH), 1.0, 0.0)


def row_pass(scale, place_ref, x_ref, warm_ref, *refs):
    *pieces, out_ref, yn_ref, beta, y_ref, e_ref, aux_ref, y_all, sums = refs
    rows, cols = x_ref.shape[1], y_ref.shape[1]
    assemble(place_ref, pieces, y_all)
    y_ref[...] = y_all[...]
    for j, part in enumerate(square_sums(y_all, TILE)):
        sl = slice(j * TILE, (j + 1) * TILE)
        yn_ref[0:1, sl] = part
        beta[0:1, sl] = warm_ref[0:1, sl] * (LOG2E / BLUR) - part * (0.5 * scale)
    sample = dot(x_ref[:, :LANES].T, y_all[:, :TILE], 1, 0) * scale + beta[0:1, :TILE]
    shift = jnp.max(sample)

    for base in range(0, rows, BIG):
        xt = x_ref[:, base : base + BIG].T
        acc = None
        for j in range(0, cols, TILE):
            b = beta[0:1, j : j + TILE] - shift
            e = jnp.exp2(dot(xt, y_all[:, j : j + TILE], 1, 0) * scale + b)
            e_ref[base : base + BIG, j : j + TILE] = e.astype(jnp.bfloat16)
            part = e[:, :LANES]
            for k in range(LANES, TILE, LANES):
                part = part + e[:, k : k + LANES]
            acc = part if acc is None else acc + part
        sums[base : base + BIG, :] = acc
    good = []
    for i in range(0, rows, LANES):
        s = jnp.sum(sums[i : i + LANES, :].T, axis=0, keepdims=True)
        good.append(in_range(s))
        out_ref[:, i : i + LANES] = jnp.broadcast_to(shift + jnp.log2(s), (out_ref.shape[0], LANES))
    ok = jnp.min(functools.reduce(jnp.minimum, good))
    aux_ref[0:1, :] = jnp.full((1, LANES), shift, jnp.float32)
    aux_ref[1:2, :] = jnp.full((1, LANES), ok, jnp.float32)

    @pl.when(ok < 0.5)
    def _():
        def slow(c, _):
            base = pl.multiple_of(c * LANES, LANES)
            xt = x_ref[:, pl.ds(base, LANES)].T

            def tile(j, state):
                top, total = state
                lane = pl.multiple_of(j * LANES, LANES)
                t = dot(xt, y_all[:, pl.ds(lane, LANES)], 1, 0) * scale + beta[0:1, pl.ds(lane, LANES)]
                new = jnp.maximum(top, t)
                return new, total * jnp.exp2(top - new) + jnp.exp2(t - new)

            first = jnp.full((LANES, LANES), -1e30, jnp.float32)
            top, total = lax.fori_loop(0, cols // LANES, tile, (first, jnp.zeros_like(first)))
            top, total = top.T, total.T
            high = jnp.max(top, axis=0, keepdims=True)
            s = jnp.sum(total * jnp.exp2(top - high), axis=0, keepdims=True)
            out_ref[:, pl.ds(base, LANES)] = jnp.broadcast_to(high + jnp.log2(s), (out_ref.shape[0], LANES))
            return 0

        lax.fori_loop(0, rows // LANES, slow, 0)


def col_pass(scale, count, x_ref, y_ref, e_ref, lg_ref, beta_ref, aux_ref, out_ref, l_ref, u_ref, pot_ref, flag_ref, u_col, l_col, total):
    rows, cols = x_ref.shape[1], y_ref.shape[1]
    l_ref[...] = lse2(lg_ref[...])
    u_ref[...] = jnp.exp2(aux_ref[0:1, 0:1] - l_ref[...])
    columns_of(u_ref, u_col)
    for j, part in enumerate(square_sums(x_ref, TILE)):
        sl = slice(j * TILE, (j + 1) * TILE)
        pot_ref[0:1, sl] = part / 512.0 - (BLUR * LN2) * l_ref[0:1, sl] + BLUR * math.log(count)

    total[...] = jnp.zeros_like(total)

    def block(i, _):
        base = pl.multiple_of(i * LANES, LANES)
        u = u_col[pl.ds(base, LANES), :]
        u = jnp.concatenate([u, u], axis=1)
        for j in range(0, cols, 2 * LANES):
            p = e_ref[pl.ds(base, LANES), j : j + 2 * LANES] * u
            while p.shape[0] > 8:
                p = p[: p.shape[0] // 2] + p[p.shape[0] // 2 :]
            total[:, j : j + 2 * LANES] += p.astype(jnp.float32)
        return 0

    lax.fori_loop(0, rows // LANES, block, 0)
    s = jnp.sum(total[...], axis=0, keepdims=True)
    ok = jnp.minimum(jnp.min(in_range(s)), jnp.min(aux_ref[1:2, :]))
    out_ref[...] = jnp.broadcast_to(jnp.log2(s) - beta_ref[...], out_ref.shape)
    flag_ref[...] = jnp.full((1, LANES), ok, jnp.float32)

    @pl.when(ok < 0.5)
    def _():
        columns_of(l_ref, l_col)

        def slow(j, _):
            lane = pl.multiple_of(j * LANES, LANES)
            y_tile = y_ref[:, pl.ds(lane, LANES)]

            def rows_of(c, state):
                top, total = state
                base = pl.multiple_of(c * LANES, LANES)
                t = dot(x_ref[:, pl.ds(base, LANES)].T, y_tile, 1, 0) * scale - l_col[pl.ds(base, LANES), :]
                new = jnp.maximum(top, t)
                return new, total * jnp.exp2(top - new) + jnp.exp2(t - new)

            first = jnp.full((LANES, LANES), -1e30, jnp.float32)
            top, total = lax.fori_loop(0, rows // LANES, rows_of, (first, jnp.zeros_like(first)))
            high = jnp.max(top, axis=0, keepdims=True)
            s = jnp.sum(total * jnp.exp2(top - high), axis=0, keepdims=True)
            out_ref[:, pl.ds(lane, LANES)] = jnp.broadcast_to(high + jnp.log2(s), (out_ref.shape[0], LANES))
            return 0

        lax.fori_loop(0, cols // LANES, slow, 0)


def mean_pass(scale, ratio, count, x_ref, y_ref, e_ref, mg_ref, l_ref, u_ref, beta_ref, yn_ref, flag_ref, out_ref, pot_ref, y_all, l_col, bias, w, den):
    rows, cols = x_ref.shape[1], y_ref.shape[1]
    features = x_ref.shape[0]
    m = lse2(mg_ref[...])
    pot_ref[...] = yn_ref[...] / 512.0 - (BLUR * LN2) * (m + ratio)
    bias[...] = math.log2(count) - m
    for j in range(0, cols, TILE):
        sl = slice(j, j + TILE)
        v = jnp.exp2(bias[0:1, sl] - beta_ref[0:1, sl]).astype(jnp.bfloat16)
        y_all[:features, sl] = y_ref[:, sl] * v
        y_all[features:, sl] = jnp.broadcast_to(v, (y_all.shape[0] - features, TILE))

    def emit(sl, num, u):
        part = num[features : features + 1] * u
        short = part.astype(jnp.bfloat16).astype(jnp.float32)
        ratio_ = jnp.where(part > 0.0, short / part, 1.0)
        out_ref[:, sl] = (num[:features] * (u * ratio_)).astype(jnp.bfloat16)
        den[0:1, sl] = short

    def chunk(c, _):
        sl = pl.ds(pl.multiple_of(c * CHUNK, CHUNK), CHUNK)
        emit(sl, dot(y_all[...], e_ref[sl, :], 1, 1), u_ref[0:1, sl])
        return 0

    lax.fori_loop(0, rows // CHUNK, chunk, 0)

    @pl.when(jnp.min(flag_ref[...]) < 0.5)
    def _():
        columns_of(l_ref, l_col)
        y_all[:features, :] = y_ref[...]
        y_all[features:, :] = jnp.ones((y_all.shape[0] - features, cols), y_all.dtype)

        def slow(c, _):
            sl = pl.ds(pl.multiple_of(c * CHUNK, CHUNK), CHUNK)
            xt = x_ref[:, sl].T

            def tile(j, _):
                lane = pl.ds(pl.multiple_of(j * LANES, LANES), LANES)
                g = dot(xt, y_all[:features, lane], 1, 0)
                w[:, lane] = jnp.exp2(g * scale + (bias[0:1, lane] - l_col[sl, :])).astype(jnp.bfloat16)
                return 0

            lax.fori_loop(0, cols // LANES, tile, 0)
            emit(sl, dot(y_all[...], w[...], 1, 1), 1.0)
            return 0

        lax.fori_loop(0, rows // CHUNK, slow, 0)

    share = out_ref.shape[0] // 16
    width = rows // share
    grid = jnp.concatenate(
        [den[0:1, k * width : (k + 1) * width] for k in range(share)], axis=0
    ).astype(jnp.bfloat16)
    for k in range(out_ref.shape[0] // share):
        out_ref[k * share : (k + 1) * share, rows : rows + width] = grid


def finish(rows, in_ref, out_ref):
    share = out_ref.shape[0]
    width = rows // share
    total = None
    for k in range(in_ref.shape[0] // share):
        part = in_ref[k * share : (k + 1) * share, :].astype(jnp.float32)
        total = part if total is None else total + part
    inverse = 1.0 / total[:, rows:]
    for k in range(share):
        sl = slice(k * width, (k + 1) * width)
        out_ref[:, sl] = (total[:, sl] * inverse[k : k + 1, :]).astype(jnp.bfloat16)


def per_device(latents, samples, warm_dual):
    n_row, n_col = lax.axis_size("row"), lax.axis_size("col")
    rows, cols = latents.shape[1], samples.shape[1]
    features = latents.shape[0] * n_col
    all_rows, all_cols = rows * n_row, cols * n_col
    scale = 2.0 * LOG2E / (2.0 * features * BLUR)
    f32, b16 = jnp.float32, jnp.bfloat16
    ring = n_row // 2
    share = samples.shape[0]
    half = share // 2

    def along(v, step):
        return lax.ppermute(v, "row", [(s, (s + 2 * step) % n_row) for s in range(n_row)])

    def swap(v):
        return lax.ppermute(v, "row", [(s, s ^ 1) for s in range(n_row)])

    low, high = samples[:half], samples[half:]
    left, left_high = along(low, 1), along(high, 1)
    right_low, right = along(low, -1), along(high, -1)
    far_low, far_high = along(left, 1), along(right, -1)
    pieces = [low, high, left, left_high, right_low, right, far_low, far_high]
    steps = [0, 0, -1, -1, 1, 1, 2, 2]
    table = np.zeros((n_row, 2 * len(steps)), np.int32)
    for r in range(n_row):
        for k, step in enumerate(steps):
            slot = ((r // 2 + step) % ring) * 2
            table[r, k] = (slot + r % 2) * share + (k % 2) * half
            table[r, k + len(steps)] = (slot + 1 - r % 2) * share + (k % 2) * half
    at = lax.dynamic_index_in_dim(jnp.asarray(table), lax.axis_index("row"), 0, keepdims=False)
    pieces = pieces + [swap(p) for p in pieces]
    x = lax.all_to_all(jnp.tile(latents, (n_col, 1)), "col", 0, 0, tiled=True)

    def like(*shape, dtype=f32):
        return jax.ShapeDtypeStruct(shape, dtype)

    l_part, yn, beta, y, e, aux = pl.pallas_call(
        functools.partial(row_pass, scale),
        out_shape=[
            like(n_col, rows),
            like(1, cols),
            like(1, cols),
            like(features, cols, dtype=b16),
            like(rows, cols, dtype=b16),
            like(2, LANES),
        ],
        in_specs=[SMEM] + [VMEM] * (2 + len(pieces)),
        out_specs=[VMEM] * 6,
        scratch_shapes=[pltpu.VMEM((features, cols), b16), pltpu.VMEM((rows, LANES), f32)],
        compiler_params=params(12),
        name="row_pass",
    )(at, x, warm_dual.reshape(1, cols), *pieces)
    l_all = lax.all_to_all(l_part, "col", 0, 0, tiled=True)
    m_part, l_sum, u, pot_lat, flag = pl.pallas_call(
        functools.partial(col_pass, scale, all_cols),
        out_shape=[like(n_row, cols), like(1, rows), like(1, rows), like(1, rows), like(1, LANES)],
        in_specs=[VMEM] * 6,
        out_specs=[VMEM] * 5,
        scratch_shapes=[pltpu.VMEM((rows, LANES), b16), pltpu.VMEM((rows, LANES), f32), pltpu.VMEM((8, cols), f32)],
        compiler_params=params(8),
        name="col_pass",
    )(x, y, e, l_all, beta, aux)
    m_all = lax.all_to_all(m_part, "row", 0, 0, tiled=True)
    num, pot_tea = pl.pallas_call(
        functools.partial(mean_pass, scale, math.log2(all_cols / all_rows), all_rows),
        out_shape=[like(features, rows + rows // latents.shape[0], dtype=b16), like(1, cols)],
        in_specs=[VMEM] * 9,
        out_specs=[VMEM] * 2,
        scratch_shapes=[
            pltpu.VMEM((features + 16, cols), b16),
            pltpu.VMEM((rows, LANES), f32),
            pltpu.VMEM((1, cols), f32),
            pltpu.VMEM((CHUNK, cols), b16),
            pltpu.VMEM((1, rows), f32),
        ],
        compiler_params=params(12),
        name="mean_pass",
    )(x, y, e, m_all, l_sum, u, beta, yn, flag)
    got = lax.all_to_all(num, "col", 0, 0, tiled=True)
    targets = pl.pallas_call(
        functools.partial(finish, rows),
        out_shape=jax.ShapeDtypeStruct((features // n_col, rows), b16),
        in_specs=[VMEM],
        out_specs=VMEM,
        compiler_params=params(4),
        name="finish",
    )(got)
    return targets, pot_lat.reshape(rows), pot_tea.reshape(cols)


def solution(mesh):
    return jax.shard_map(
        per_device,
        mesh=mesh,
        in_specs=(P("col", "row"), P("row", "col"), P("col")),
        out_specs=(P("col", "row"), P("row"), P("col")),
        check_vma=False,
    )
```
